32 devices in a mesh: row: 8 (over y, x, core), col: 4 (over z).
Axes of the slice: x: 2, y: 2, z: 4, core: 2. Of those that a mesh axis runs over, the one named last changes fastest.
Arguments:
- features: bfloat16 [16384, 512], P(('row', 'col')), may hold values from -6 to 6
- weight: bfloat16 [512, 512], replicated, may hold values from -0.25 to 0.25
- bias: float32 [512], replicated, may hold values from -3 to 3
- cotangent: bfloat16 [16384, 512], P(('row', 'col')), may hold values from -6 to 6
- tile_values: bfloat16 [8, 4, 64, 128, 128], P('row', 'col'), may hold values from -0.1875 to 0.1875
- tile_rows: int32 [8, 4, 64], P('row', 'col'), may hold values from 0 to 127, as said below
- tile_cols: int32 [8, 4, 64], P('row', 'col'), may hold values from 0 to 127, as said below
- tile_counts: int32 [8, 4], P('row', 'col'), may hold values from 1 to 64
Outputs:
- output: bfloat16 [16384, 512], P(('row', 'col'))
- feature_grad: bfloat16 [16384, 512], P(('row', 'col'))
- weight_grad: float32 [512, 512], replicated
- bias_grad: float32 [512], replicated
The draws below stay inside these ranges and needn't reach their ends.
Inputs may be any that keep to these rules, and one draw needn't show every extreme that they name: `tile_rows`: A tile on device (p, q) has its row block in row group p, that is row block // 16 == p, and its column block's atoms on devices of index q along col, that is (column block // 4) % 4 == q. The rows of features held by device (p, q) are blocks p * 4 * 4 + q * 4 to that plus 4 - 1. Row and column pairs may repeat. `tile_cols`: among one device's live tiles at most 16 have their row block held by any one device of that row group, and at most 8 have their column block held by any one device of that column group.
All inputs are finite; a program needn't handle non-finite values.
Results may differ from the reference program's by a relative error of at most 0.013.
Values may be sent and summed in bfloat16 or wider, within the bound.
A program may use at most 128 MiB of HBM per device.

```python
import math
import jax
import jax.numpy as jnp
from jax import lax

D = 512
BS = 128
BLK_DEV = 4
KMAX = 64
BLOCKS = 128
ATOMS = 16384
N_ROW = 8
N_COL = 4


def slot_order(sub_key):
    return jax.random.permutation(sub_key, KMAX)


def tile_layout(key):
    base_key = jax.random.fold_in(key, 4711)
    key_list = jax.random.split(base_key, 5)
    device_total = N_ROW * N_COL
    full_device = jax.random.randint(key_list[0], (), 0, device_total)
    partial_counts = jax.random.randint(key_list[1], (device_total,), KMAX // 4, 3 * KMAX // 4 + 1)
    counts = jnp.where(jnp.arange(device_total) == full_device, KMAX, partial_counts).astype(jnp.int32)
    orders = jax.vmap(slot_order)(jax.random.split(key_list[2], device_total)).astype(jnp.int32)
    row_owner = orders % N_ROW
    col_owner = (orders // N_ROW + orders) % N_COL
    device_ids = jnp.arange(device_total, dtype=jnp.int32)
    device_rows = (device_ids // N_COL)[:, None]
    device_cols = (device_ids % N_COL)[:, None]
    row_pick = jax.random.randint(key_list[3], (device_total, KMAX), 0, BLK_DEV)
    col_pick = jax.random.randint(key_list[4], (device_total, KMAX), 0, BLK_DEV)
    rows = device_rows * (BLK_DEV * N_COL) + col_owner * BLK_DEV + row_pick
    cols = row_owner * (BLK_DEV * N_COL) + device_cols * BLK_DEV + col_pick
    return (rows.reshape(N_ROW, N_COL, KMAX).astype(jnp.int32), cols.reshape(N_ROW, N_COL, KMAX).astype(jnp.int32), counts.reshape(N_ROW, N_COL))


def draw_tile_rows(key, part):
    return tile_layout(key)[0]


def draw_tile_cols(key, part):
    return tile_layout(key)[1]


def draw_tile_counts(key, part):
    return tile_layout(key)[2]


def shard_levels(stream_key, dims, pieces, low, top_value):
    factor_of, own = 1.0, jax.random.fold_in(stream_key, 6)
    for dim, blocks in pieces:
        draws = jnp.exp(jax.random.uniform(jax.random.fold_in(own, dim), (blocks,), jnp.float32, low / len(pieces), top_value / len(pieces)))
        factor_of = factor_of * jnp.repeat(draws, dims[dim] // blocks).reshape([-1 if axis == dim else 1 for axis in range(len(dims))])
    return factor_of


def scatter_about(key, extent, scale, reach, cuts=(), kind=jnp.bfloat16):
    loudness = shard_levels(key, extent, cuts, -0.22, 0.18) if cuts else 1.0
    drawn = jax.random.normal(key, extent, jnp.float32) * scale * loudness
    return jnp.minimum(jnp.maximum(drawn, -reach), reach).astype(kind)


def setup_inputs(seed: int = 0) -> dict:
    keys = jax.random.split(jax.random.key(seed), 9)
    features = scatter_about(keys[0], (ATOMS, D), 1.0, 6.0, ((0, 32),))
    weight = scatter_about(keys[1], (D, D), D ** -0.5, 0.25)
    bias = scatter_about(keys[2], (D,), 0.5, 3.0, (), jnp.float32)
    cotangent = scatter_about(keys[3], (ATOMS, D), 1.0, 6.0, ((0, 32),))
    tile_values = scatter_about(keys[4], (N_ROW, N_COL, KMAX, BS, BS), (8 * BS) ** -0.5, 0.1875, ((0, 8), (1, 4)))
    tile_rows = draw_tile_rows(jax.random.fold_in(keys[8], 71), 0)
    tile_cols = draw_tile_cols(jax.random.fold_in(keys[8], 71), 0)
    tile_counts = draw_tile_counts(jax.random.fold_in(keys[8], 71), 0)
    return dict(features=features, weight=weight, bias=bias, cotangent=cotangent, tile_values=tile_values, tile_rows=tile_rows, tile_cols=tile_cols, tile_counts=tile_counts)


def block_products(tiles, alive, source_blocks, fetch_ids, add_ids, transpose):

    def step(carry, items):
        tile_group, fetch_row, add_row, alive_row = items
        picked = source_blocks[fetch_row].astype(jnp.float32)
        mats = tile_group.astype(jnp.float32)
        if transpose:
            products = jnp.einsum('kba,kbd->kad', mats, picked)
        else:
            products = jnp.einsum('kab,kbd->kad', mats, picked)
        products = products * alive_row.astype(jnp.float32)[:, None, None]
        return (carry.at[add_row].add(products), None)
    initial = jnp.zeros((BLOCKS, BS, D), jnp.float32)
    total, unused = lax.scan(step, initial, (tiles, fetch_ids, add_ids, alive))
    return total.reshape(ATOMS, D)

def reference(features, weight, bias, cotangent, tile_values, tile_rows, tile_cols, tile_counts):
    device_total = N_ROW * N_COL
    tiles = tile_values.reshape(device_total, KMAX, BS, BS)
    row_ids = tile_rows.reshape(device_total, KMAX).astype(jnp.int32)
    col_ids = tile_cols.reshape(device_total, KMAX).astype(jnp.int32)
    alive = jnp.arange(KMAX, dtype=jnp.int32)[None, :] < tile_counts.reshape(device_total, 1)
    feature_blocks = features.reshape(BLOCKS, BS, D)
    aggregated = block_products(tiles, alive, feature_blocks, col_ids, row_ids, False).astype(jnp.bfloat16)
    pre_act = jnp.dot(aggregated, weight, preferred_element_type=jnp.float32) + bias.astype(jnp.float32)
    sigm = jax.nn.sigmoid(pre_act)
    output = (pre_act * sigm).astype(jnp.bfloat16)
    grad_pre = (cotangent.astype(jnp.float32) * sigm * (1.0 + pre_act * (1.0 - sigm))).astype(jnp.bfloat16)
    scale = 1.0 / math.sqrt(ATOMS)
    weight_grad = jnp.dot(aggregated.T, grad_pre, preferred_element_type=jnp.float32) * scale
    bias_grad = lax.optimization_barrier(jnp.sum(grad_pre.astype(jnp.float32), axis=0)) * scale
    grad_agg = jnp.dot(grad_pre, weight.T, preferred_element_type=jnp.float32).astype(jnp.bfloat16)
    grad_blocks = grad_agg.reshape(BLOCKS, BS, D)
    feature_grad = block_products(tiles, alive, grad_blocks, row_ids, col_ids, True).astype(jnp.bfloat16)
    return (output, feature_grad, weight_grad, bias_grad)
```

```python
import functools
import math

import jax
import jax.numpy as jnp
from jax import lax
from jax.experimental import pallas as pl
from jax.experimental.pallas import tpu as pltpu
from jax.sharding import PartitionSpec as P

MESH = pl.DeviceIdType.MESH
BF = jnp.bfloat16
F32 = jnp.float32
PAD = 16


def flip(k, bits):
    out = k
    for b in range(8):
        step = 1 << b
        if bits & step:
            out = out + step - 2 * step * ((k // step) % 2)
    return out


def remote(src, dst, send, recv, to):
    return pltpu.make_async_remote_copy(
        src_ref=src, dst_ref=dst, send_sem=send, recv_sem=recv, device_id=to, device_id_type=MESH
    )


def greet(peers):
    barrier = pltpu.get_barrier_semaphore()
    for peer in peers:
        pl.semaphore_signal(barrier, inc=1, device_id=peer, device_id_type=MESH)
    pl.semaphore_wait(barrier, len(peers))


def gather_kernel(chips, nb, feats, out, held, own_sem, s_same, r_same, s_part, r_part):
    r, q = lax.axis_index("row"), lax.axis_index("col")
    k, c = r // 2, r % 2
    hb = nb // 2
    relay = chips == 4
    near = [d for d in range(1, chips) if not (relay and d == 3)]
    partner = (k * 2 + 1 - c, q)

    def dev(d):
        return (flip(k, d) * 2 + c, q)

    def slot(d, core, h):
        return out.at[pl.ds((flip(k, d) * 2 + core) * nb + h * hb, hb)]

    def own(d, h):
        return remote(
            feats.at[pl.ds(h * hb, hb)], slot(0, c, h), s_same.at[d, h], r_same.at[d, h], dev(d)
        )

    def pass_on(h):
        via, to = (1, 2) if h == 0 else (2, 1)
        return remote(slot(via, c, h), slot(via, c, h), s_same.at[3, h], r_same.at[3, h], dev(to))

    def inc(d, h):
        return remote(slot(d, c, h), slot(d, c, h), s_same.at[d, h], r_same.at[d, h], dev(d))

    def fwd(d, h):
        src = feats.at[pl.ds(h * hb, hb)] if d == 0 else slot(d, c, h)
        return remote(src, slot(d, c, h), s_part.at[d, h], r_part.at[d, h], partner)

    def inc_part(d, h):
        return remote(
            slot(d, 1 - c, h), slot(d, 1 - c, h), s_part.at[d, h], r_part.at[d, h], partner
        )

    greet([partner] + [dev(d) for d in near])
    take = pltpu.make_async_copy(feats, held, own_sem.at[0])
    take.start()
    for n in range(2):
        for d in near:
            own(d, (n + (d == 2)) % 2).start()
    for h in range(2):
        fwd(0, h).start()
    take.wait()
    put = pltpu.make_async_copy(held, out.at[pl.ds(r * nb, nb)], own_sem.at[1])
    put.start()
    for n in range(2):
        for d in near:
            h = (n + (d == 2)) % 2
            inc(d, h).wait_recv()
            if relay and n == 0:
                pass_on(h).start()
            fwd(d, h).start()
    if relay:
        for h in range(2):
            inc(3, h).wait_recv()
            fwd(3, h).start()
    for d in range(chips):
        for h in range(2):
            inc_part(d, h).wait_recv()
    for h in range(2):
        for d in near:
            own(d, h).wait_send()
        if relay:
            pass_on(h).wait_send()
        for d in range(chips):
            fwd(d, h).wait_send()
    put.wait()


def tile_kernel(
    back, group, blk, ncol, counts, rows, cols, tiles, src, out, lists, lens, acc
):
    slots, size = tiles.shape[0], tiles.shape[1]
    dests = out.shape[0]
    span = blk * ncol

    def row_id(k):
        return rows[k] % span

    def col_id(k):
        g = cols[k]
        return g // span * blk + g % blk

    dst_of, src_of = (col_id, row_id) if back else (row_id, col_id)

    @pl.loop(0, dests)
    def _(d):
        lens[d] = 0

    @pl.loop(0, counts[0])
    def _(k):
        d = dst_of(k)
        n = lens[d]
        lists[d * slots + n] = k
        lens[d] = n + 1

    @pl.loop(0, dests)
    def _(d):
        m = lens[d]
        acc[...] = jnp.zeros_like(acc)

        @pl.loop(0, (m + group - 1) // group)
        def _(t):
            left, right = [], []
            for i in range(group):
                at = t * group + i
                k = lists[d * slots + jnp.minimum(at, m - 1)]
                mat = tiles[k]
                left.append(jnp.where(at < m, mat, jnp.zeros_like(mat)))
                right.append(src[src_of(k)])
            lhs = jnp.concatenate(left, axis=0 if back else 1)
            rhs = jnp.concatenate(right, axis=0)
            dims = (((0,), (0,)), ((), ())) if back else (((1,), (0,)), ((), ()))
            acc[...] += lax.dot_general(lhs, rhs, dims, preferred_element_type=F32)

        out[d] = acc[...].astype(BF)


def middle_kernel(
    n, nb, scale, part, w, bias, cot, out, spread, wp,
    acc_r, acc_l, agg, gp, accf, s_r, r_r, s_l, r_l, s_gr, r_gr, s_gl, r_gl,
):
    r, q = lax.axis_index("row"), lax.axis_index("col")
    last = n - 1
    right, left = (r, jnp.minimum(q + 1, last)), (r, jnp.maximum(q - 1, 0))
    size = part.shape[1]

    def chain(buf, s, v, to, d, j, first=False):
        at = d * nb + j
        return remote(
            (part if first else buf).at[at], buf.at[at], s.at[d, j], v.at[d, j], to
        )

    cp_r = functools.partial(chain, acc_r, s_r, r_r, right)
    cp_l = functools.partial(chain, acc_l, s_l, r_l, left)

    def cp_g(s, v, to, d, j):
        at = d * nb + j
        return remote(spread.at[at], spread.at[at], s.at[d, j], v.at[d, j], to)

    cp_gr = functools.partial(cp_g, s_gr, r_gr, right)
    cp_gl = functools.partial(cp_g, s_gl, r_gl, left)

    def hop(cp, buf, mine, start, d, j):
        @pl.when(mine)
        def _():
            @pl.when(start)
            def _():
                cp(d, j, True).start()

            @pl.when(jnp.logical_not(start))
            def _():
                cp(d, j).wait_recv()
                at = d * nb + j
                buf[at] = (buf[at].astype(F32) + part[at].astype(F32)).astype(BF)
                cp(d, j).start()

    def reduce_block(j):
        for i in range(n - 1):
            hop(cp_r, acc_r, q < last - i, q == 0, last - i, j)
            hop(cp_l, acc_l, q > i, q == last, i, j)

    def finish_block(j):
        at = q * nb + j
        accf[...] = part[at].astype(F32)

        @pl.when(q > 0)
        def _():
            cp_r(q, j).wait_recv()
            accf[...] += acc_r[at].astype(F32)

        @pl.when(q < last)
        def _():
            cp_l(q, j).wait_recv()
            accf[...] += acc_l[at].astype(F32)

        rows = pl.ds(j * size, size)
        a = accf[...].astype(BF)
        agg[rows, :] = a
        pre = jnp.dot(a, w[...], preferred_element_type=F32) + bias[...]
        sig = jax.nn.sigmoid(pre)
        out[rows, :] = (pre * sig).astype(BF)
        g = (cot[rows, :].astype(F32) * sig * (1.0 + pre * (1.0 - sig))).astype(BF)
        gp[rows, :] = g
        spread[at] = lax.dot_general(
            g, w[...], (((1,), (1,)), ((), ())), preferred_element_type=F32
        ).astype(BF)

        @pl.when(q < last)
        def _():
            cp_gr(q, j).start()

        @pl.when(q > 0)
        def _():
            cp_gl(q, j).start()

    def relay_block(j):
        for o in range(1, n):
            @pl.when(q >= o)
            def _():
                cp_gr(q - o, j).wait_recv()

                @pl.when(q < last)
                def _():
                    cp_gr(q - o, j).start()

            @pl.when(q + o <= last)
            def _():
                cp_gl(q + o, j).wait_recv()

                @pl.when(q > 0)
                def _():
                    cp_gl(q + o, j).start()

    barrier = pltpu.get_barrier_semaphore()

    @pl.when(q > 0)
    def _():
        pl.semaphore_signal(barrier, inc=1, device_id=left, device_id_type=MESH)

    @pl.when(q < last)
    def _():
        pl.semaphore_signal(barrier, inc=1, device_id=right, device_id_type=MESH)

    pl.semaphore_wait(barrier, jnp.minimum(q, 1) + jnp.minimum(last - q, 1))

    for step in range(nb + 3):
        if step < nb:
            reduce_block(step)
        if 0 <= step - 1 < nb:
            finish_block(step - 1)
        if 0 <= step - 3 < nb:
            if step == nb + 2:
                weight_block(n, scale, agg, gp, wp)
            relay_block(step - 3)

    for j in range(nb):
        for d in range(n):
            @pl.when(q < d)
            def _():
                cp_r(d, j).wait_send()

            @pl.when(q > d)
            def _():
                cp_l(d, j).wait_send()

            @pl.when(jnp.logical_and(q >= d, q < last))
            def _():
                cp_gr(d, j).wait_send()

            @pl.when(jnp.logical_and(q <= d, q > 0))
            def _():
                cp_gl(d, j).wait_send()


def weight_block(n, scale, agg, gp, wp):
    width = agg.shape[1]
    rows = width // (2 * n)
    total = jnp.sum(gp[...].astype(F32), axis=0, keepdims=True) * scale
    pad = jnp.broadcast_to(total, (PAD, width)).astype(BF)
    step = 128
    for t in range(width // step):
        res = lax.dot_general(
            agg[:, t * step : (t + 1) * step],
            gp[...],
            (((0,), (0,)), ((), ())),
            preferred_element_type=F32,
        )
        res = (res * scale).astype(BF)
        for u in range(step // rows):
            p = (t * step) // rows + u
            wp[p // n, p % n, :rows, :] = res[u * rows : (u + 1) * rows]
            wp[p // n, p % n, rows:, :] = pad


def add_rows(dst, srcs, begin, count):
    step = 64

    @pl.loop(0, count // step)
    def _(i):
        at = pl.ds(pl.multiple_of(begin + i * step, step), step)
        total = srcs[0][at, :].astype(F32)
        for s in srcs[1:]:
            total = total + s[at, :].astype(F32)
        dst[at, :] = total.astype(dst.dtype)


def final_kernel(
    chips, n, part, wp, fg, wg, bg, a_buf, b_buf, c_buf, w1, w2, w3, w4,
    s_a, r_a, s_b, r_b, s_c, r_c, s_w1, r_w1, s_w2, r_w2, s_w3, r_w3, s_w4, r_w4, s_w5, r_w5,
):
    r, q = lax.axis_index("row"), lax.axis_index("col")
    k, c = r // 2, r % 2
    relay = chips == 4
    near = [d for d in range(1, chips) if not (relay and d == 3)]
    partner = (k * 2 + 1 - c, q)
    rows = part.shape[1]
    half = rows // 2

    def dev(d):
        return (flip(k, d) * 2 + c, q)

    def deep(dz):
        return (r, (q + dz) % n)

    def mine(d):
        return part.at[flip(k, d) * 2 + c]

    def cp_a(d):
        return remote(
            part.at[flip(k, d) * 2 + 1 - c], a_buf.at[d], s_a.at[d], r_a.at[d], partner
        )

    def cp_b(d, h):
        at = pl.ds(h * half, half)
        return remote(a_buf.at[d, at], b_buf.at[d, at], s_b.at[d, h], r_b.at[d, h], dev(d))

    def cp_c(h):
        return remote(
            a_buf.at[3, pl.ds(h * half, half)], c_buf.at[h], s_c.at[h], r_c.at[h], dev(h + 1)
        )

    cp_w1 = remote(wp.at[1 - c], w1, s_w1.at[0], r_w1.at[0], partner)

    def cp_w2(dz):
        return remote(w1.at[(q + dz) % n], w2.at[dz], s_w2.at[dz], r_w2.at[dz], deep(dz))

    def cp_w3(d):
        return remote(w3.at[k], w3.at[k], s_w3.at[d], r_w3.at[d], dev(d))

    def cp_w4(dz):
        return remote(w4.at[c, q], w4.at[c, q], s_w4.at[dz], r_w4.at[dz], deep(dz))

    def cp_w5(dz):
        at = (q + n - dz) % n
        return remote(w4.at[c, at], w4.at[c, at], s_w5.at[dz], r_w5.at[dz], partner)

    greet([partner] + [dev(d) for d in range(1, chips)] + [deep(dz) for dz in range(1, n)])
    cp_w1.start()
    order = list(range(chips - 1, 0, -1)) + [0]
    if relay:
        order = [3, 1, 2, 0]
    for d in order:
        cp_a(d).start()

    def join(d):
        cp_a(d).wait_recv()
        add_rows(a_buf.at[d], [a_buf.at[d], mine(d)], 0, rows)

    if relay:
        join(3)
        cp_c(0).start()
        cp_c(1).start()
        join(1)
        cp_b(1, 0).start()
        join(2)
        cp_b(2, 1).start()
    else:
        for d in order[:-1]:
            join(d)
            for h in range(2):
                cp_b(d, h).start()

    cp_w1.wait_recv()
    for z in range(n):
        w1[z] = (w1[z].astype(F32) + wp[c, z].astype(F32)).astype(BF)
    for dz in range(1, n):
        cp_w2(dz).start()

    if relay:
        cp_c(0).wait_recv()
        add_rows(a_buf.at[2], [a_buf.at[2], c_buf.at[0]], 0, half)
        cp_b(2, 0).start()
        cp_c(1).wait_recv()

        @pl.loop(0, half // 64)
        def _(i):
            at = pl.ds(pl.multiple_of(half + i * 64, 64), 64)
            lo = pl.ds(pl.multiple_of(i * 64, 64), 64)
            a_buf[1, at, :] = (
                a_buf[1, at, :].astype(F32) + c_buf[1, lo, :].astype(F32)
            ).astype(BF)

        cp_b(1, 1).start()

    total = w1[q].astype(F32)
    for dz in range(1, n):
        cp_w2(dz).wait_recv()
        total = total + w2[dz].astype(F32)
    w3[k] = total.astype(BF)
    for d in range(1, chips):
        cp_w3(d).start()
    cp_a(0).wait_recv()
    for d in range(1, chips):
        other = flip(k, d)
        remote(w3.at[other], w3.at[other], s_w3.at[d], r_w3.at[d], dev(d)).wait_recv()
    total = w3[0].astype(F32)
    for i in range(1, chips):
        total = total + w3[i].astype(F32)
    w4[c, q] = total.astype(BF)
    for dz in range(1, n):
        cp_w4(dz).start()
    cp_w5(0).start()
    for dz in range(1, n):
        at = (q + n - dz) % n
        remote(
            w4.at[c, at], w4.at[c, at], s_w4.at[dz], r_w4.at[dz], deep(dz)
        ).wait_recv()
        cp_w5(dz).start()

    for d in near:
        for h in range(2):
            cp_b(d, h).wait_recv()
    add_rows(fg, [a_buf.at[0], mine(0)] + [b_buf.at[d] for d in near], 0, rows)

    for dz in range(n):
        at = (q + n - dz) % n
        remote(
            w4.at[1 - c, at], w4.at[1 - c, at], s_w5.at[dz], r_w5.at[dz], partner
        ).wait_recv()
    take = w4.shape[2] - PAD
    for i in range(2):
        for z in range(n):
            p = i * n + z
            wg[p * take : (p + 1) * take, :] = w4[i, z, :take, :].astype(F32)
    bg[...] = w4[0, 0, take:, :].astype(F32)[:8]

    cp_w1.wait_send()
    for d in range(chips):
        cp_a(d).wait_send()
    for d in near:
        for h in range(2):
            cp_b(d, h).wait_send()
    if relay:
        for h in range(2):
            cp_c(h).wait_send()
    for d in range(1, chips):
        cp_w3(d).wait_send()
    for dz in range(n):
        if dz:
            cp_w2(dz).wait_send()
            cp_w4(dz).wait_send()
        cp_w5(dz).wait_send()


VM = pl.BlockSpec(memory_space=pltpu.VMEM)
SM = pl.BlockSpec(memory_space=pltpu.SMEM)
ANY = pl.BlockSpec(memory_space=pl.ANY)


def params(cid):
    return pltpu.CompilerParams(collective_id=cid, has_side_effects=True)


def dma(*shape):
    return pltpu.SemaphoreType.DMA(shape)


def run_tiles(back, group, blk, ncol, dests, counts, rows, cols, values, src):
    slots, size = values.shape[0], values.shape[1]
    width = src.shape[2]
    return pl.pallas_call(
        functools.partial(tile_kernel, back, group, blk, ncol),
        out_shape=jax.ShapeDtypeStruct((dests, size, width), BF),
        in_specs=[SM, SM, SM, VM, VM],
        out_specs=VM,
        scratch_shapes=[
            pltpu.SMEM((dests * slots,), jnp.int32),
            pltpu.SMEM((dests,), jnp.int32),
            pltpu.VMEM((size, width), F32),
        ],
        name="tiles_back" if back else "tiles_fwd",
    )(counts, rows, cols, values, src)


def on_device(features, weight, bias, cotangent, tile_values, tile_rows, tile_cols, tile_counts):
    nrow = lax.axis_size("row")
    ncol = lax.axis_size("col")
    node_dev, width = features.shape
    slots, size = tile_values.shape[2], tile_values.shape[3]
    nb = node_dev // size
    chips = nrow // 2
    scale = 1.0 / math.sqrt(node_dev * nrow * ncol)
    values = tile_values.reshape(slots, size, size)
    rows, cols = tile_rows.reshape(slots), tile_cols.reshape(slots)
    counts = tile_counts.reshape(1)

    gathered = pl.pallas_call(
        functools.partial(gather_kernel, chips, nb),
        out_shape=jax.ShapeDtypeStruct((nrow * nb, size, width), BF),
        in_specs=[ANY],
        out_specs=ANY,
        scratch_shapes=[pltpu.VMEM((nb, size, width), BF), dma(2)] + [dma(chips, 2)] * 4,
        compiler_params=params(0),
        name="gather",
    )(features.reshape(nb, size, width))

    partial = run_tiles(False, 4, nb, ncol, ncol * nb, counts, rows, cols, values, gathered)

    pr = width // (2 * ncol) + PAD
    out, spread, wp = pl.pallas_call(
        functools.partial(middle_kernel, ncol, nb, scale),
        out_shape=[
            jax.ShapeDtypeStruct((node_dev, width), BF),
            jax.ShapeDtypeStruct((ncol * nb, size, width), BF),
            jax.ShapeDtypeStruct((2, ncol, pr, width), BF),
        ],
        in_specs=[VM] * 4,
        out_specs=[VM] * 3,
        scratch_shapes=[
            pltpu.VMEM((ncol * nb, size, width), BF),
            pltpu.VMEM((ncol * nb, size, width), BF),
            pltpu.VMEM((node_dev, width), BF),
            pltpu.VMEM((node_dev, width), BF),
            pltpu.VMEM((size, width), F32),
        ]
        + [dma(ncol, nb)] * 8,
        compiler_params=params(1),
        name="middle",
    )(partial, weight, bias.reshape(1, width), cotangent)

    grads = run_tiles(True, 2, nb, ncol, nrow * nb, counts, rows, cols, values, spread)

    fg, wg, bg = pl.pallas_call(
        functools.partial(final_kernel, chips, ncol),
        out_shape=[
            jax.ShapeDtypeStruct((node_dev, width), BF),
            jax.ShapeDtypeStruct((width, width), F32),
            jax.ShapeDtypeStruct((8, width), F32),
        ],
        in_specs=[VM] * 2,
        out_specs=[VM] * 3,
        scratch_shapes=[
            pltpu.VMEM((chips, node_dev, width), BF),
            pltpu.VMEM((chips, node_dev, width), BF),
            pltpu.VMEM((2, node_dev // 2, width), BF),
            pltpu.VMEM((ncol, pr, width), BF),
            pltpu.VMEM((ncol, pr, width), BF),
            pltpu.VMEM((chips, pr, width), BF),
            pltpu.VMEM((2, ncol, pr, width), BF),
            dma(chips), dma(chips), dma(chips, 2), dma(chips, 2), dma(2), dma(2),
            dma(1), dma(1), dma(ncol), dma(ncol), dma(chips), dma(chips),
            dma(ncol), dma(ncol), dma(ncol), dma(ncol),
        ],
        compiler_params=params(2),
        name="final",
    )(grads.reshape(nrow, node_dev, width), wp)
    return (out, fg, wg, bg[0])


def solution(mesh):
    return jax.shard_map(
        on_device,
        mesh=mesh,
        in_specs=(
            P(("row", "col"), None),
            P(),
            P(),
            P(("row", "col"), None),
            P("row", "col", None, None, None),
            P("row", "col", None),
            P("row", "col", None),
            P("row", "col"),
        ),
        out_specs=(P(("row", "col"), None), P(("row", "col"), None), P(), P()),
        check_vma=False,
    )
```

```python
import functools
import math

import jax
import jax.numpy as jnp
from jax import lax
from jax.experimental import pallas as pl
from jax.experimental.pallas import tpu as pltpu
from jax.sharding import PartitionSpec as P

MESH = pl.DeviceIdType.MESH
BF = jnp.bfloat16
F32 = jnp.float32
PAD = 16


def flip(k, bits):
    out = k
    for b in range(8):
        step = 1 << b
        if bits & step:
            out = out + step - 2 * step * ((k // step) % 2)
    return out


def remote(src, dst, send, recv, to):
    return pltpu.make_async_remote_copy(
        src_ref=src, dst_ref=dst, send_sem=send, recv_sem=recv, device_id=to, device_id_type=MESH
    )


def greet(peers):
    barrier = pltpu.get_barrier_semaphore()
    for peer in peers:
        pl.semaphore_signal(barrier, inc=1, device_id=peer, device_id_type=MESH)
    pl.semaphore_wait(barrier, len(peers))


def gather_kernel(chips, nb, feats, out, held, own_sem, s_same, r_same, s_part, r_part):
    r, q = lax.axis_index("row"), lax.axis_index("col")
    k, c = r // 2, r % 2
    hb = nb // 2
    relay = chips == 4
    near = [d for d in range(1, chips) if not (relay and d == 3)]
    partner = (k * 2 + 1 - c, q)

    def dev(d):
        return (flip(k, d) * 2 + c, q)

    def slot(d, core, h):
        return out.at[pl.ds((flip(k, d) * 2 + core) * nb + h * hb, hb)]

    def own(d, h):
        return remote(
            feats.at[pl.ds(h * hb, hb)], slot(0, c, h), s_same.at[d, h], r_same.at[d, h], dev(d)
        )

    def pass_on(h):
        via, to = (1, 2) if h == 0 else (2, 1)
        return remote(slot(via, c, h), slot(via, c, h), s_same.at[3, h], r_same.at[3, h], dev(to))

    def inc(d, h):
        return remote(slot(d, c, h), slot(d, c, h), s_same.at[d, h], r_same.at[d, h], dev(d))

    def fwd(d, h):
        src = feats.at[pl.ds(h * hb, hb)] if d == 0 else slot(d, c, h)
        return remote(src, slot(d, c, h), s_part.at[d, h], r_part.at[d, h], partner)

    def inc_part(d, h):
        return remote(
            slot(d, 1 - c, h), slot(d, 1 - c, h), s_part.at[d, h], r_part.at[d, h], partner
        )

    greet([partner] + [dev(d) for d in near])
    take = pltpu.make_async_copy(feats, held, own_sem.at[0])
    take.start()
    for n in range(2):
        for d in near:
            own(d, (n + (d == 2)) % 2).start()
    for h in range(2):
        fwd(0, h).start()
    take.wait()
    put = pltpu.make_async_copy(held, out.at[pl.ds(r * nb, nb)], own_sem.at[1])
    put.start()
    for n in range(2):
        for d in near:
            h = (n + (d == 2)) % 2
            inc(d, h).wait_recv()
            if relay and n == 0:
                pass_on(h).start()
            fwd(d, h).start()
    if relay:
        for h in range(2):
            inc(3, h).wait_recv()
            fwd(3, h).start()
    for d in range(chips):
        for h in range(2):
            inc_part(d, h).wait_recv()
    for h in range(2):
        for d in near:
            own(d, h).wait_send()
        if relay:
            pass_on(h).wait_send()
        for d in range(chips):
            fwd(d, h).wait_send()
    put.wait()


def tile_kernel(
    back, group, blk, ncol, counts, rows, cols, tiles, src, out, lists, lens, acc
):
    slots, size = tiles.shape[0], tiles.shape[1]
    dests = out.shape[0]
    span = blk * ncol

    def row_id(k):
        return rows[k] % span

    def col_id(k):
        g = cols[k]
        return g // span * blk + g % blk

    dst_of, src_of = (col_id, row_id) if back else (row_id, col_id)

    @pl.loop(0, dests)
    def _(d):
        lens[d] = 0

    @pl.loop(0, counts[0])
    def _(k):
        d = dst_of(k)
        n = lens[d]
        lists[d * slots + n] = k
        lens[d] = n + 1

    @pl.loop(0, dests)
    def _(d):
        m = lens[d]
        acc[...] = jnp.zeros_like(acc)

        @pl.loop(0, (m + group - 1) // group)
        def _(t):
            left, right = [], []
            for i in range(group):
                at = t * group + i
                k = lists[d * slots + jnp.minimum(at, m - 1)]
                mat = tiles[k]
                left.append(jnp.where(at < m, mat, jnp.zeros_like(mat)))
                right.append(src[src_of(k)])
            lhs = jnp.concatenate(left, axis=0 if back else 1)
            rhs = jnp.concatenate(right, axis=0)
            dims = (((0,), (0,)), ((), ())) if back else (((1,), (0,)), ((), ()))
            acc[...] += lax.dot_general(lhs, rhs, dims, preferred_element_type=F32)

        out[d] = acc[...].astype(BF)


def middle_kernel(
    n, chips, np_, scale, part, w, bias, cot, out, spread, ws,
    acc_r, acc_l, agg, gp, accf, wp, w1, w2,
    s_r, r_r, s_l, r_l, s_gr, r_gr, s_gl, r_gl, s_w1, r_w1, s_w2, r_w2,
):
    r, q = lax.axis_index("row"), lax.axis_index("col")
    k, c = r // 2, r % 2
    last = n - 1
    right, left = (r, jnp.minimum(q + 1, last)), (r, jnp.maximum(q - 1, 0))
    partner = (k * 2 + 1 - c, q)
    size = part.shape[1]

    def dev(d):
        return (flip(k, d) * 2 + c, q)

    def chain(buf, s, v, to, d, j, first=False):
        at = d * np_ + j
        return remote(
            (part if first else buf).at[at], buf.at[at], s.at[d, j], v.at[d, j], to
        )

    cp_r = functools.partial(chain, acc_r, s_r, r_r, right)
    cp_l = functools.partial(chain, acc_l, s_l, r_l, left)

    def cp_g(s, v, to, d, j):
        at = d * np_ + j
        return remote(spread.at[at], spread.at[at], s.at[d, j], v.at[d, j], to)

    cp_gr = functools.partial(cp_g, s_gr, r_gr, right)
    cp_gl = functools.partial(cp_g, s_gl, r_gl, left)
    cp_w1 = remote(wp.at[1 - c], w1, s_w1.at[0], r_w1.at[0], partner)

    def cp_w2(d):
        return remote(w1.at[flip(k, d)], w2.at[d], s_w2.at[d], r_w2.at[d], dev(d))

    def hop(cp, buf, start, d, j):
        @pl.when(start)
        def _():
            cp(d, j, True).start()

        @pl.when(jnp.logical_not(start))
        def _():
            cp(d, j).wait_recv()
            at = d * np_ + j
            buf[at] = (buf[at].astype(F32) + part[at].astype(F32)).astype(BF)
            cp(d, j).start()

    def live(j):
        return jnp.logical_and(j >= 0, j < np_)

    def reduce_step(t):
        jr, jl = t - q, t - (last - q)

        @pl.when(live(jr))
        def _():
            @pl.loop(0, last - q)
            def _(i):
                hop(cp_r, acc_r, q == 0, last - i, jr)

        @pl.when(live(jl))
        def _():
            @pl.loop(0, q)
            def _(i):
                hop(cp_l, acc_l, q == last, i, jl)

    def finish(j):
        at = q * np_ + j
        accf[...] = part[at].astype(F32)

        @pl.when(q > 0)
        def _():
            cp_r(q, j).wait_recv()
            accf[...] += acc_r[at].astype(F32)

        @pl.when(q < last)
        def _():
            cp_l(q, j).wait_recv()
            accf[...] += acc_l[at].astype(F32)

        rows = pl.ds(pl.multiple_of(j * size, size), size)
        a = accf[...].astype(BF)
        agg[rows, :] = a
        pre = jnp.dot(a, w[...], preferred_element_type=F32) + bias[...]
        sig = jax.nn.sigmoid(pre)
        out[rows, :] = (pre * sig).astype(BF)
        g = (cot[rows, :].astype(F32) * sig * (1.0 + pre * (1.0 - sig))).astype(BF)
        gp[rows, :] = g
        spread[at] = lax.dot_general(
            g, w[...], (((1,), (1,)), ((), ())), preferred_element_type=F32
        ).astype(BF)

        @pl.when(q < last)
        def _():
            cp_gr(q, j).start()

        @pl.when(q > 0)
        def _():
            cp_gl(q, j).start()

    def relay(j, o):
        @pl.when(jnp.logical_and(live(j), q >= o))
        def _():
            cp_gr(q - o, j).wait_recv()

            @pl.when(q < last)
            def _():
                cp_gr(q - o, j).start()

        @pl.when(jnp.logical_and(live(j), q + o <= last))
        def _():
            cp_gl(q + o, j).wait_recv()

            @pl.when(q > 0)
            def _():
                cp_gl(q + o, j).start()

    barrier = pltpu.get_barrier_semaphore()
    peers = [partner] + [dev(d) for d in range(1, chips)]
    for peer in peers:
        pl.semaphore_signal(barrier, inc=1, device_id=peer, device_id_type=MESH)

    @pl.when(q > 0)
    def _():
        pl.semaphore_signal(barrier, inc=1, device_id=left, device_id_type=MESH)

    @pl.when(q < last)
    def _():
        pl.semaphore_signal(barrier, inc=1, device_id=right, device_id_type=MESH)

    pl.semaphore_wait(barrier, jnp.minimum(q, 1) + jnp.minimum(last - q, 1) + len(peers))

    @pl.loop(0, np_ + 2 * last)
    def _(t):
        reduce_step(t)
        for o in range(1, n):
            relay(t - last - o, o)

        @pl.when(live(t - last))
        def _():
            finish(t - last)

        @pl.when(t == np_ - 1 + last)
        def _():
            weight_block(chips, scale, agg, gp, wp)
            cp_w1.start()

        @pl.when(t == np_ - 1 + last + 1)
        def _():
            cp_w1.wait_recv()
            for z in range(chips):
                w1[z] = (w1[z].astype(F32) + wp[c, z].astype(F32)).astype(BF)
            for d in range(1, chips):
                cp_w2(d).start()

    total = w1[k].astype(F32)
    for d in range(1, chips):
        cp_w2(d).wait_recv()
        total = total + w2[d].astype(F32)
    ws[...] = total.astype(BF)

    @pl.loop(0, np_)
    def _(j):
        for d in range(n):
            @pl.when(q < d)
            def _():
                cp_r(d, j).wait_send()

            @pl.when(q > d)
            def _():
                cp_l(d, j).wait_send()

            @pl.when(jnp.logical_and(q >= d, q < last))
            def _():
                cp_gr(d, j).wait_send()

            @pl.when(jnp.logical_and(q <= d, q > 0))
            def _():
                cp_gl(d, j).wait_send()

    cp_w1.wait_send()
    for d in range(1, chips):
        cp_w2(d).wait_send()


def weight_block(parts, scale, agg, gp, wp):
    width = agg.shape[1]
    rows = width // (2 * parts)
    total = jnp.sum(gp[...].astype(F32), axis=0, keepdims=True) * scale
    pad = jnp.broadcast_to(total, (PAD, width)).astype(BF)
    step = 128
    for t in range(width // step):
        res = lax.dot_general(
            agg[:, t * step : (t + 1) * step],
            gp[...],
            (((0,), (0,)), ((), ())),
            preferred_element_type=F32,
        )
        res = (res * scale).astype(BF)
        for u in range(step // rows):
            p = (t * step) // rows + u
            wp[p // parts, p % parts, :rows, :] = res[u * rows : (u + 1) * rows]
            wp[p // parts, p % parts, rows:, :] = pad


def add_rows(dst, srcs, begin, count):
    step = 64

    @pl.loop(0, count // step)
    def _(i):
        at = pl.ds(pl.multiple_of(begin + i * step, step), step)
        total = srcs[0][at, :].astype(F32)
        for s in srcs[1:]:
            total = total + s[at, :].astype(F32)
        dst[at, :] = total.astype(dst.dtype)


def final_kernel(
    chips, n, part, ws, fg, w4, a_buf, b_buf, c_buf, w3,
    s_a, r_a, s_b, r_b, s_c, r_c, s_w3, r_w3, s_w4, r_w4, s_w5, r_w5,
):
    r, q = lax.axis_index("row"), lax.axis_index("col")
    k, c = r // 2, r % 2
    relay = chips == 4
    near = [d for d in range(1, chips) if not (relay and d == 3)]
    partner = (k * 2 + 1 - c, q)
    rows = part.shape[1]
    half = rows // 2

    def dev(d):
        return (flip(k, d) * 2 + c, q)

    def deep(dz):
        return (r, (q + dz) % n)

    def mine(d):
        return part.at[flip(k, d) * 2 + c]

    def cp_a(d):
        return remote(
            part.at[flip(k, d) * 2 + 1 - c], a_buf.at[d], s_a.at[d], r_a.at[d], partner
        )

    def cp_b(d, h):
        at = pl.ds(h * half, half)
        return remote(a_buf.at[d, at], b_buf.at[d, at], s_b.at[d, h], r_b.at[d, h], dev(d))

    def cp_c(h):
        return remote(
            a_buf.at[3, pl.ds(h * half, half)], c_buf.at[h], s_c.at[h], r_c.at[h], dev(h + 1)
        )

    def cp_w3(dz):
        return remote(ws, w3.at[q], s_w3.at[dz], r_w3.at[dz], deep(dz))

    def cp_w4(d):
        return remote(w4.at[c, k], w4.at[c, k], s_w4.at[d], r_w4.at[d], dev(d))

    def cp_w5(d):
        at = flip(k, d)
        return remote(w4.at[c, at], w4.at[c, at], s_w5.at[d], r_w5.at[d], partner)

    greet([partner] + [dev(d) for d in range(1, chips)] + [deep(dz) for dz in range(1, n)])
    order = list(range(chips - 1, 0, -1)) + [0]
    if relay:
        order = [3, 1, 2, 0]
    for d in order:
        cp_a(d).start()
    for dz in range(1, n):
        cp_w3(dz).start()

    def join(d):
        cp_a(d).wait_recv()
        add_rows(a_buf.at[d], [a_buf.at[d], mine(d)], 0, rows)

    if relay:
        join(3)
        cp_c(0).start()
        cp_c(1).start()
        join(1)
        cp_b(1, 0).start()
        join(2)
        cp_b(2, 1).start()
    else:
        for d in order[:-1]:
            join(d)
            for h in range(2):
                cp_b(d, h).start()

    w3[q] = ws[...]
    for dz in range(1, n):
        at = (q + n - dz) % n
        remote(w3.at[at], w3.at[at], s_w3.at[dz], r_w3.at[dz], deep(dz)).wait_recv()
    total = w3[0].astype(F32)
    for i in range(1, n):
        total = total + w3[i].astype(F32)
    w4[c, k] = total.astype(BF)
    for d in range(1, chips):
        cp_w4(d).start()
    cp_w5(0).start()

    if relay:
        cp_c(0).wait_recv()
        add_rows(a_buf.at[2], [a_buf.at[2], c_buf.at[0]], 0, half)
        cp_b(2, 0).start()
        cp_c(1).wait_recv()
        at = pl.ds(half, half)
        add_rows(a_buf.at[1, at], [a_buf.at[1, at], c_buf.at[1]], 0, half)
        cp_b(1, 1).start()

    join(0)
    for d in range(1, chips):
        at = flip(k, d)
        remote(w4.at[c, at], w4.at[c, at], s_w4.at[d], r_w4.at[d], dev(d)).wait_recv()
        cp_w5(d).start()
    for h in range(2):
        for d in near:
            cp_b(d, (h + (d == 2)) % 2).wait_recv()
    add_rows(fg, [a_buf.at[0]] + [b_buf.at[d] for d in near], 0, rows)

    for d in range(chips):
        at = flip(k, d)
        remote(
            w4.at[1 - c, at], w4.at[1 - c, at], s_w5.at[d], r_w5.at[d], partner
        ).wait_recv()

    for d in range(chips):
        cp_a(d).wait_send()
        cp_w5(d).wait_send()
    for d in near:
        for h in range(2):
            cp_b(d, h).wait_send()
    if relay:
        for h in range(2):
            cp_c(h).wait_send()
    for d in range(1, chips):
        cp_w4(d).wait_send()
    for dz in range(1, n):
        cp_w3(dz).wait_send()


VM = pl.BlockSpec(memory_space=pltpu.VMEM)
SM = pl.BlockSpec(memory_space=pltpu.SMEM)
ANY = pl.BlockSpec(memory_space=pl.ANY)


def params(cid):
    return pltpu.CompilerParams(collective_id=cid, has_side_effects=True)


def dma(*shape):
    return pltpu.SemaphoreType.DMA(shape)


def run_tiles(back, group, blk, ncol, dests, counts, rows, cols, values, src):
    slots, size = values.shape[0], values.shape[1]
    width = src.shape[2]
    return pl.pallas_call(
        functools.partial(tile_kernel, back, group, blk, ncol),
        out_shape=jax.ShapeDtypeStruct((dests, size, width), BF),
        in_specs=[SM, SM, SM, VM, VM],
        out_specs=VM,
        scratch_shapes=[
            pltpu.SMEM((dests * slots,), jnp.int32),
            pltpu.SMEM((dests,), jnp.int32),
            pltpu.VMEM((size, width), F32),
        ],
        name="tiles_back" if back else "tiles_fwd",
    )(counts, rows, cols, values, src)


def on_device(features, weight, bias, cotangent, tile_values, tile_rows, tile_cols, tile_counts):
    nrow = lax.axis_size("row")
    ncol = lax.axis_size("col")
    node_dev, width = features.shape
    slots, size = tile_values.shape[2], tile_values.shape[3]
    nb = node_dev // size
    chips = nrow // 2
    scale = 1.0 / math.sqrt(node_dev * nrow * ncol)
    values = tile_values.reshape(slots, size, size)
    rows, cols = tile_rows.reshape(slots), tile_cols.reshape(slots)
    counts = tile_counts.reshape(1)

    gathered = pl.pallas_call(
        functools.partial(gather_kernel, chips, nb),
        out_shape=jax.ShapeDtypeStruct((nrow * nb, size, width), BF),
        in_specs=[ANY],
        out_specs=ANY,
        scratch_shapes=[pltpu.VMEM((nb, size, width), BF), dma(2)] + [dma(chips, 2)] * 4,
        compiler_params=params(0),
        name="gather",
    )(features.reshape(nb, size, width))

    partial = run_tiles(False, 4, nb, ncol, ncol * nb, counts, rows, cols, values, gathered)

    part_rows = width // (2 * chips)
    pr = part_rows + PAD
    piece = size // 2
    pieces = node_dev // piece
    wide = (ncol * pieces, piece, width)
    out, spread, ws = pl.pallas_call(
        functools.partial(middle_kernel, ncol, chips, pieces, scale),
        out_shape=[
            jax.ShapeDtypeStruct((node_dev, width), BF),
            jax.ShapeDtypeStruct(wide, BF),
            jax.ShapeDtypeStruct((pr, width), BF),
        ],
        in_specs=[VM] * 4,
        out_specs=[VM] * 3,
        scratch_shapes=[
            pltpu.VMEM(wide, BF),
            pltpu.VMEM(wide, BF),
            pltpu.VMEM((node_dev, width), BF),
            pltpu.VMEM((node_dev, width), BF),
            pltpu.VMEM((piece, width), F32),
            pltpu.VMEM((2, chips, pr, width), BF),
            pltpu.VMEM((chips, pr, width), BF),
            pltpu.VMEM((chips, pr, width), BF),
        ]
        + [dma(ncol, pieces)] * 8
        + [dma(1), dma(1), dma(chips), dma(chips)],
        compiler_params=params(1),
        name="middle",
    )(partial.reshape(wide), weight, bias.reshape(1, width), cotangent)
    spread = spread.reshape(ncol * nb, size, width)

    grads = run_tiles(True, 2, nb, ncol, nrow * nb, counts, rows, cols, values, spread)

    fg, parts = pl.pallas_call(
        functools.partial(final_kernel, chips, ncol),
        out_shape=[
            jax.ShapeDtypeStruct((node_dev, width), BF),
            jax.ShapeDtypeStruct((2, chips, pr, width), BF),
        ],
        in_specs=[VM] * 2,
        out_specs=[VM] * 2,
        scratch_shapes=[
            pltpu.VMEM((chips, node_dev, width), BF),
            pltpu.VMEM((chips, node_dev, width), BF),
            pltpu.VMEM((2, node_dev // 2, width), BF),
            pltpu.VMEM((ncol, pr, width), BF),
            dma(chips), dma(chips), dma(chips, 2), dma(chips, 2), dma(2), dma(2),
            dma(ncol), dma(ncol), dma(chips), dma(chips), dma(chips), dma(chips),
        ],
        compiler_params=params(2),
        name="final",
    )(grads.reshape(nrow, node_dev, width), ws)
    wg = parts[:, :, :part_rows].astype(F32).reshape(width, width)
    bg = parts[0, 0, part_rows].astype(F32)
    return (out, fg, wg, bg)


def solution(mesh):
    return jax.shard_map(
        on_device,
        mesh=mesh,
        in_specs=(
            P(("row", "col"), None),
            P(),
            P(),
            P(("row", "col"), None),
            P("row", "col", None, None, None),
            P("row", "col", None),
            P("row", "col", None),
            P("row", "col"),
        ),
        out_specs=(P(("row", "col"), None), P(("row", "col"), None), P(), P()),
        check_vma=False,
    )
```

```python
import functools
import math

import jax
import jax.numpy as jnp
from jax import lax
from jax.experimental import pallas as pl
from jax.experimental.pallas import tpu as pltpu
from jax.sharding import PartitionSpec as P

MESH = pl.DeviceIdType.MESH
BF = jnp.bfloat16
F32 = jnp.float32
PAD = 16
WAYS = 2


def flip(k, bits):
    out = k
    for b in range(8):
        step = 1 << b
        if bits & step:
            out = out + step - 2 * step * ((k // step) % 2)
    return out


def remote(src, dst, send, recv, to):
    return pltpu.make_async_remote_copy(
        src_ref=src, dst_ref=dst, send_sem=send, recv_sem=recv, device_id=to, device_id_type=MESH
    )


def greet(peers):
    barrier = pltpu.get_barrier_semaphore()
    for peer in peers:
        pl.semaphore_signal(barrier, inc=1, device_id=peer, device_id_type=MESH)
    pl.semaphore_wait(barrier, len(peers))


def gather_kernel(chips, nb, feats, out, held, own_sem, s_same, r_same, s_part, r_part):
    r, q = lax.axis_index("row"), lax.axis_index("col")
    k, c = r // 2, r % 2
    hb = nb // 2
    relay = chips == 4
    near = [d for d in range(1, chips) if not (relay and d == 3)]
    partner = (k * 2 + 1 - c, q)

    def dev(d):
        return (flip(k, d) * 2 + c, q)

    def slot(d, core, h):
        return out.at[pl.ds((flip(k, d) * 2 + core) * nb + h * hb, hb)]

    def own(d, h):
        return remote(
            feats.at[pl.ds(h * hb, hb)], slot(0, c, h), s_same.at[d, h], r_same.at[d, h], dev(d)
        )

    def pass_on(h):
        via, to = (1, 2) if h == 0 else (2, 1)
        return remote(slot(via, c, h), slot(via, c, h), s_same.at[3, h], r_same.at[3, h], dev(to))

    def inc(d, h):
        return remote(slot(d, c, h), slot(d, c, h), s_same.at[d, h], r_same.at[d, h], dev(d))

    def fwd(d, h):
        src = feats.at[pl.ds(h * hb, hb)] if d == 0 else slot(d, c, h)
        return remote(src, slot(d, c, h), s_part.at[d, h], r_part.at[d, h], partner)

    def inc_part(d, h):
        return remote(
            slot(d, 1 - c, h), slot(d, 1 - c, h), s_part.at[d, h], r_part.at[d, h], partner
        )

    greet([partner] + [dev(d) for d in near])
    take = pltpu.make_async_copy(feats, held, own_sem.at[0])
    take.start()
    for n in range(2):
        for d in near:
            own(d, (n + (d == 2)) % 2).start()
    for h in range(2):
        fwd(0, h).start()
    take.wait()
    put = pltpu.make_async_copy(held, out.at[pl.ds(r * nb, nb)], own_sem.at[1])
    put.start()
    for n in range(2):
        for d in near:
            h = (n + (d == 2)) % 2
            inc(d, h).wait_recv()
            if relay and n == 0:
                pass_on(h).start()
            fwd(d, h).start()
    if relay:
        for h in range(2):
            inc(3, h).wait_recv()
            fwd(3, h).start()
    for d in range(chips):
        for h in range(2):
            inc_part(d, h).wait_recv()
    for h in range(2):
        for d in near:
            own(d, h).wait_send()
        if relay:
            pass_on(h).wait_send()
        for d in range(chips):
            fwd(d, h).wait_send()
    put.wait()


def tile_kernel(
    back, group, blk, ncol, counts, rows, cols, tiles, src, out, lists, lens, acc
):
    slots, size = tiles.shape[0], tiles.shape[1]
    dests = out.shape[0]
    span = blk * ncol

    def row_id(k):
        return rows[k] % span

    def col_id(k):
        g = cols[k]
        return g // span * blk + g % blk

    dst_of, src_of = (col_id, row_id) if back else (row_id, col_id)

    @pl.loop(0, dests)
    def _(d):
        lens[d] = 0

    @pl.loop(0, counts[0])
    def _(k):
        d = dst_of(k)
        n = lens[d]
        lists[d * slots + n] = k
        lens[d] = n + 1

    def product(d, m, t):
        left, right = [], []
        for i in range(group):
            at = t * group + i
            k = jnp.where(at < m, lists[d * slots + jnp.minimum(at, slots - 1)], 0)
            mat = tiles[k]
            left.append(jnp.where(at < m, mat, jnp.zeros_like(mat)))
            right.append(src[src_of(k)])
        lhs = jnp.concatenate(left, axis=0 if back else 1)
        rhs = jnp.concatenate(right, axis=0)
        dims = (((0,), (0,)), ((), ())) if back else (((1,), (0,)), ((), ()))
        return lax.dot_general(lhs, rhs, dims, preferred_element_type=F32)

    @pl.loop(0, dests // WAYS)
    def _(e):
        ids = [e * WAYS + i for i in range(WAYS)]
        sizes = [lens[d] for d in ids]
        most = functools.reduce(jnp.maximum, sizes)
        for i in range(WAYS):
            acc[i] = product(ids[i], sizes[i], 0)

        @pl.loop(1, (most + group - 1) // group)
        def _(t):
            for i in range(WAYS):
                acc[i] = acc[i] + product(ids[i], sizes[i], t)

        for i in range(WAYS):
            out[ids[i]] = acc[i].astype(BF)


def middle_kernel(
    n, chips, np_, scale, part, w, bias, cot, out, spread, ws,
    acc_r, acc_l, agg, gp, accf, wp, w1, w2,
    s_r, r_r, s_l, r_l, s_gr, r_gr, s_gl, r_gl, s_w1, r_w1, s_w2, r_w2,
):
    r, q = lax.axis_index("row"), lax.axis_index("col")
    k, c = r // 2, r % 2
    last = n - 1
    right, left = (r, jnp.minimum(q + 1, last)), (r, jnp.maximum(q - 1, 0))
    partner = (k * 2 + 1 - c, q)
    size = part.shape[1]

    def dev(d):
        return (flip(k, d) * 2 + c, q)

    def chain(buf, s, v, to, d, j, first=False):
        at = d * np_ + j
        return remote(
            (part if first else buf).at[at], buf.at[at], s.at[d, j], v.at[d, j], to
        )

    cp_r = functools.partial(chain, acc_r, s_r, r_r, right)
    cp_l = functools.partial(chain, acc_l, s_l, r_l, left)

    def cp_g(s, v, to, d, j):
        at = d * np_ + j
        return remote(spread.at[at], spread.at[at], s.at[d, j], v.at[d, j], to)

    cp_gr = functools.partial(cp_g, s_gr, r_gr, right)
    cp_gl = functools.partial(cp_g, s_gl, r_gl, left)
    cp_w1 = remote(wp.at[1 - c], w1, s_w1.at[0], r_w1.at[0], partner)

    def cp_w2(d):
        return remote(w1.at[flip(k, d)], w2.at[d], s_w2.at[d], r_w2.at[d], dev(d))

    def hop(cp, buf, start, d, j):
        @pl.when(start)
        def _():
            cp(d, j, True).start()

        @pl.when(jnp.logical_not(start))
        def _():
            cp(d, j).wait_recv()
            at = d * np_ + j
            buf[at] = (buf[at].astype(F32) + part[at].astype(F32)).astype(BF)
            cp(d, j).start()

    def live(j):
        return jnp.logical_and(j >= 0, j < np_)

    def reduce_step(t):
        jr, jl = t - q, t - (last - q)

        @pl.when(live(jr))
        def _():
            @pl.loop(0, last - q)
            def _(i):
                hop(cp_r, acc_r, q == 0, last - i, jr)

        @pl.when(live(jl))
        def _():
            @pl.loop(0, q)
            def _(i):
                hop(cp_l, acc_l, q == last, i, jl)

    def finish(j):
        at = q * np_ + j
        accf[...] = part[at].astype(F32)

        @pl.when(q > 0)
        def _():
            cp_r(q, j).wait_recv()
            accf[...] += acc_r[at].astype(F32)

        @pl.when(q < last)
        def _():
            cp_l(q, j).wait_recv()
            accf[...] += acc_l[at].astype(F32)

        rows = pl.ds(pl.multiple_of(j * size, size), size)
        a = accf[...].astype(BF)
        agg[rows, :] = a
        pre = jnp.dot(a, w[...], preferred_element_type=F32) + bias[...]
        sig = jax.nn.sigmoid(pre)
        out[rows, :] = (pre * sig).astype(BF)
        g = (cot[rows, :].astype(F32) * sig * (1.0 + pre * (1.0 - sig))).astype(BF)
        gp[rows, :] = g
        spread[at] = lax.dot_general(
            g, w[...], (((1,), (1,)), ((), ())), preferred_element_type=F32
        ).astype(BF)

        @pl.when(q < last)
        def _():
            cp_gr(q, j).start()

        @pl.when(q > 0)
        def _():
            cp_gl(q, j).start()

    def relay(j, o):
        @pl.when(jnp.logical_and(live(j), q >= o))
        def _():
            cp_gr(q - o, j).wait_recv()

            @pl.when(q < last)
            def _():
                cp_gr(q - o, j).start()

        @pl.when(jnp.logical_and(live(j), q + o <= last))
        def _():
            cp_gl(q + o, j).wait_recv()

            @pl.when(q > 0)
            def _():
                cp_gl(q + o, j).start()

    barrier = pltpu.get_barrier_semaphore()
    peers = [partner] + [dev(d) for d in range(1, chips)]
    for peer in peers:
        pl.semaphore_signal(barrier, inc=1, device_id=peer, device_id_type=MESH)

    @pl.when(q > 0)
    def _():
        pl.semaphore_signal(barrier, inc=1, device_id=left, device_id_type=MESH)

    @pl.when(q < last)
    def _():
        pl.semaphore_signal(barrier, inc=1, device_id=right, device_id_type=MESH)

    pl.semaphore_wait(barrier, jnp.minimum(q, 1) + jnp.minimum(last - q, 1) + len(peers))

    @pl.loop(0, np_ + 2 * last)
    def _(t):
        reduce_step(t)
        for o in range(1, n):
            relay(t - last - o, o)

        @pl.when(live(t - last))
        def _():
            finish(t - last)

        @pl.when(t == np_ - 1 + last)
        def _():
            weight_block(chips, scale, agg, gp, wp)
            cp_w1.start()

        @pl.when(t == np_ - 1 + last + 1)
        def _():
            cp_w1.wait_recv()
            for z in range(chips):
                w1[z] = (w1[z].astype(F32) + wp[c, z].astype(F32)).astype(BF)
            for d in range(1, chips):
                cp_w2(d).start()

    total = w1[k].astype(F32)
    for d in range(1, chips):
        cp_w2(d).wait_recv()
        total = total + w2[d].astype(F32)
    ws[...] = total.astype(BF)

    @pl.loop(0, np_)
    def _(j):
        for d in range(n):
            @pl.when(q < d)
            def _():
                cp_r(d, j).wait_send()

            @pl.when(q > d)
            def _():
                cp_l(d, j).wait_send()

            @pl.when(jnp.logical_and(q >= d, q < last))
            def _():
                cp_gr(d, j).wait_send()

            @pl.when(jnp.logical_and(q <= d, q > 0))
            def _():
                cp_gl(d, j).wait_send()

    cp_w1.wait_send()
    for d in range(1, chips):
        cp_w2(d).wait_send()


def weight_block(parts, scale, agg, gp, wp):
    width = agg.shape[1]
    rows = width // (2 * parts)
    total = jnp.sum(gp[...].astype(F32), axis=0, keepdims=True) * scale
    pad = jnp.broadcast_to(total, (PAD, width)).astype(BF)
    step = 128
    for t in range(width // step):
        res = lax.dot_general(
            agg[:, t * step : (t + 1) * step],
            gp[...],
            (((0,), (0,)), ((), ())),
            preferred_element_type=F32,
        )
        res = (res * scale).astype(BF)
        for u in range(step // rows):
            p = (t * step) // rows + u
            wp[p // parts, p % parts, :rows, :] = res[u * rows : (u + 1) * rows]
            wp[p // parts, p % parts, rows:, :] = pad


def add_rows(dst, srcs, begin, count):
    step = 64

    @pl.loop(0, count // step)
    def _(i):
        at = pl.ds(pl.multiple_of(begin + i * step, step), step)
        total = srcs[0][at, :].astype(F32)
        for s in srcs[1:]:
            total = total + s[at, :].astype(F32)
        dst[at, :] = total.astype(dst.dtype)


def final_kernel(
    chips, n, part, ws, fg, w4, bg, a_buf, b_buf, c_buf, w3,
    s_a, r_a, s_b, r_b, s_c, r_c, s_w3, r_w3, s_w4, r_w4, s_w5, r_w5,
):
    r, q = lax.axis_index("row"), lax.axis_index("col")
    k, c = r // 2, r % 2
    relay = chips == 4
    near = [d for d in range(1, chips) if not (relay and d == 3)]
    partner = (k * 2 + 1 - c, q)
    rows = part.shape[1]
    half = rows // 2

    def dev(d):
        return (flip(k, d) * 2 + c, q)

    def deep(dz):
        return (r, (q + dz) % n)

    def mine(d):
        return part.at[flip(k, d) * 2 + c]

    def cp_a(d):
        return remote(
            part.at[flip(k, d) * 2 + 1 - c], a_buf.at[d], s_a.at[d], r_a.at[d], partner
        )

    def cp_b(d, h):
        at = pl.ds(h * half, half)
        return remote(a_buf.at[d, at], b_buf.at[d, at], s_b.at[d, h], r_b.at[d, h], dev(d))

    def cp_c(h):
        return remote(
            a_buf.at[3, pl.ds(h * half, half)], c_buf.at[h], s_c.at[h], r_c.at[h], dev(h + 1)
        )

    def cp_w3(dz):
        return remote(ws, w3.at[q], s_w3.at[dz], r_w3.at[dz], deep(dz))

    def cp_w4(d):
        return remote(w4.at[c, k], w4.at[c, k], s_w4.at[d], r_w4.at[d], dev(d))

    def cp_w5(d):
        at = flip(k, d)
        return remote(w4.at[c, at], w4.at[c, at], s_w5.at[d], r_w5.at[d], partner)

    greet([partner] + [dev(d) for d in range(1, chips)] + [deep(dz) for dz in range(1, n)])
    order = list(range(chips - 1, 0, -1)) + [0]
    if relay:
        order = [3, 1, 2, 0]
    for d in order:
        cp_a(d).start()
    for dz in range(1, n):
        cp_w3(dz).start()

    def join(d):
        cp_a(d).wait_recv()
        add_rows(a_buf.at[d], [a_buf.at[d], mine(d)], 0, rows)

    if relay:
        join(3)
        cp_c(0).start()
        cp_c(1).start()
        join(1)
        cp_b(1, 0).start()
        join(2)
        cp_b(2, 1).start()
    else:
        for d in order[:-1]:
            join(d)
            for h in range(2):
                cp_b(d, h).start()

    w3[q] = ws[...]
    for dz in range(1, n):
        at = (q + n - dz) % n
        remote(w3.at[at], w3.at[at], s_w3.at[dz], r_w3.at[dz], deep(dz)).wait_recv()
    total = w3[0].astype(F32)
    for i in range(1, n):
        total = total + w3[i].astype(F32)
    w4[c, k] = total.astype(BF)
    for d in range(1, chips):
        cp_w4(d).start()
    cp_w5(0).start()

    if relay:
        cp_c(0).wait_recv()
        add_rows(a_buf.at[2], [a_buf.at[2], c_buf.at[0]], 0, half)
        cp_b(2, 0).start()
        cp_c(1).wait_recv()
        at = pl.ds(half, half)
        add_rows(a_buf.at[1, at], [a_buf.at[1, at], c_buf.at[1]], 0, half)
        cp_b(1, 1).start()

    join(0)
    for d in range(1, chips):
        at = flip(k, d)
        remote(w4.at[c, at], w4.at[c, at], s_w4.at[d], r_w4.at[d], dev(d)).wait_recv()
        cp_w5(d).start()
    for h in range(2):
        for d in near:
            cp_b(d, (h + (d == 2)) % 2).wait_recv()
    add_rows(fg, [a_buf.at[0]] + [b_buf.at[d] for d in near], 0, rows)

    for d in range(chips):
        at = flip(k, d)
        remote(
            w4.at[1 - c, at], w4.at[1 - c, at], s_w5.at[d], r_w5.at[d], partner
        ).wait_recv()

    bg[...] = w4[0, 0, w4.shape[2] - PAD :, :].astype(F32)[:1]
    for d in range(chips):
        cp_a(d).wait_send()
        cp_w5(d).wait_send()
    for d in near:
        for h in range(2):
            cp_b(d, h).wait_send()
    if relay:
        for h in range(2):
            cp_c(h).wait_send()
    for d in range(1, chips):
        cp_w4(d).wait_send()
    for dz in range(1, n):
        cp_w3(dz).wait_send()


VM = pl.BlockSpec(memory_space=pltpu.VMEM)
SM = pl.BlockSpec(memory_space=pltpu.SMEM)
ANY = pl.BlockSpec(memory_space=pl.ANY)


def params(cid):
    return pltpu.CompilerParams(collective_id=cid, has_side_effects=True)


def dma(*shape):
    return pltpu.SemaphoreType.DMA(shape)


def run_tiles(back, group, blk, ncol, dests, counts, rows, cols, values, src):
    slots, size = values.shape[0], values.shape[1]
    width = src.shape[2]
    return pl.pallas_call(
        functools.partial(tile_kernel, back, group, blk, ncol),
        out_shape=jax.ShapeDtypeStruct((dests, size, width), BF),
        in_specs=[SM, SM, SM, VM, VM],
        out_specs=VM,
        scratch_shapes=[
            pltpu.SMEM((dests * slots,), jnp.int32),
            pltpu.SMEM((dests,), jnp.int32),
            pltpu.VMEM((WAYS, size, width), F32),
        ],
        name="tiles_back" if back else "tiles_fwd",
    )(counts, rows, cols, values, src)


def on_device(features, weight, bias, cotangent, tile_values, tile_rows, tile_cols, tile_counts):
    nrow = lax.axis_size("row")
    ncol = lax.axis_size("col")
    node_dev, width = features.shape
    slots, size = tile_values.shape[2], tile_values.shape[3]
    nb = node_dev // size
    chips = nrow // 2
    scale = 1.0 / math.sqrt(node_dev * nrow * ncol)
    values = tile_values.reshape(slots, size, size)
    rows, cols = tile_rows.reshape(slots), tile_cols.reshape(slots)
    counts = tile_counts.reshape(1)

    gathered = pl.pallas_call(
        functools.partial(gather_kernel, chips, nb),
        out_shape=jax.ShapeDtypeStruct((nrow * nb, size, width), BF),
        in_specs=[ANY],
        out_specs=ANY,
        scratch_shapes=[pltpu.VMEM((nb, size, width), BF), dma(2)] + [dma(chips, 2)] * 4,
        compiler_params=params(0),
        name="gather",
    )(features.reshape(nb, size, width))

    partial = run_tiles(False, 4, nb, ncol, ncol * nb, counts, rows, cols, values, gathered)

    part_rows = width // (2 * chips)
    pr = part_rows + PAD
    piece = size // 4
    pieces = node_dev // piece
    wide = (ncol * pieces, piece, width)
    out, spread, ws = pl.pallas_call(
        functools.partial(middle_kernel, ncol, chips, pieces, scale),
        out_shape=[
            jax.ShapeDtypeStruct((node_dev, width), BF),
            jax.ShapeDtypeStruct(wide, BF),
            jax.ShapeDtypeStruct((pr, width), BF),
        ],
        in_specs=[VM] * 4,
        out_specs=[VM] * 3,
        scratch_shapes=[
            pltpu.VMEM(wide, BF),
            pltpu.VMEM(wide, BF),
            pltpu.VMEM((node_dev, width), BF),
            pltpu.VMEM((node_dev, width), BF),
            pltpu.VMEM((piece, width), F32),
            pltpu.VMEM((2, chips, pr, width), BF),
            pltpu.VMEM((chips, pr, width), BF),
            pltpu.VMEM((chips, pr, width), BF),
        ]
        + [dma(ncol, pieces)] * 8
        + [dma(1), dma(1), dma(chips), dma(chips)],
        compiler_params=params(1),
        name="middle",
    )(partial.reshape(wide), weight, bias.reshape(1, width), cotangent)
    spread = spread.reshape(ncol * nb, size, width)

    grads = run_tiles(True, 2, nb, ncol, nrow * nb, counts, rows, cols, values, spread)

    fg, parts, bg = pl.pallas_call(
        functools.partial(final_kernel, chips, ncol),
        out_shape=[
            jax.ShapeDtypeStruct((node_dev, width), BF),
            jax.ShapeDtypeStruct((2, chips, pr, width), BF),
            jax.ShapeDtypeStruct((1, width), F32),
        ],
        in_specs=[VM] * 2,
        out_specs=[VM] * 3,
        scratch_shapes=[
            pltpu.VMEM((chips, node_dev, width), BF),
            pltpu.VMEM((chips, node_dev, width), BF),
            pltpu.VMEM((2, node_dev // 2, width), BF),
            pltpu.VMEM((ncol, pr, width), BF),
            dma(chips), dma(chips), dma(chips, 2), dma(chips, 2), dma(2), dma(2),
            dma(ncol), dma(ncol), dma(chips), dma(chips), dma(chips), dma(chips),
        ],
        compiler_params=params(2),
        name="final",
    )(grads.reshape(nrow, node_dev, width), ws)
    wg = parts[:, :, :part_rows].astype(F32).reshape(width, width)
    return (out, fg, wg, bg.reshape(width))


def solution(mesh):
    return jax.shard_map(
        on_device,
        mesh=mesh,
        in_specs=(
            P(("row", "col"), None),
            P(),
            P(),
            P(("row", "col"), None),
            P("row", "col", None, None, None),
            P("row", "col", None),
            P("row", "col", None),
            P("row", "col"),
        ),
        out_specs=(P(("row", "col"), None), P(("row", "col"), None), P(), P()),
        check_vma=False,
    )
```

```python
import functools
import math

import jax
import jax.numpy as jnp
from jax import lax
from jax.experimental import pallas as pl
from jax.experimental.pallas import tpu as pltpu
from jax.sharding import PartitionSpec as P

MESH = pl.DeviceIdType.MESH
BF = jnp.bfloat16
F32 = jnp.float32
PAD = 16
WAYS = 2


def flip(k, bits):
    out = k
    for b in range(8):
        step = 1 << b
        if bits & step:
            out = out + step - 2 * step * ((k // step) % 2)
    return out


def remote(src, dst, send, recv, to):
    return pltpu.make_async_remote_copy(
        src_ref=src, dst_ref=dst, send_sem=send, recv_sem=recv, device_id=to, device_id_type=MESH
    )


def greet(peers):
    barrier = pltpu.get_barrier_semaphore()
    for peer in peers:
        pl.semaphore_signal(barrier, inc=1, device_id=peer, device_id_type=MESH)
    pl.semaphore_wait(barrier, len(peers))


def gather_kernel(chips, nb, feats, out, held, own_sem, s_same, r_same, s_part, r_part):
    r, q = lax.axis_index("row"), lax.axis_index("col")
    k, c = r // 2, r % 2
    hb = nb // 2
    relay = chips == 4
    near = [d for d in range(1, chips) if not (relay and d == 3)]
    partner = (k * 2 + 1 - c, q)

    def dev(d):
        return (flip(k, d) * 2 + c, q)

    def slot(d, core, h):
        return out.at[pl.ds((flip(k, d) * 2 + core) * nb + h * hb, hb)]

    def own(d, h):
        return remote(
            feats.at[pl.ds(h * hb, hb)], slot(0, c, h), s_same.at[d, h], r_same.at[d, h], dev(d)
        )

    def pass_on(h):
        via, to = (1, 2) if h == 0 else (2, 1)
        return remote(slot(via, c, h), slot(via, c, h), s_same.at[3, h], r_same.at[3, h], dev(to))

    def inc(d, h):
        return remote(slot(d, c, h), slot(d, c, h), s_same.at[d, h], r_same.at[d, h], dev(d))

    def fwd(d, h):
        src = feats.at[pl.ds(h * hb, hb)] if d == 0 else slot(d, c, h)
        return remote(src, slot(d, c, h), s_part.at[d, h], r_part.at[d, h], partner)

    def inc_part(d, h):
        return remote(
            slot(d, 1 - c, h), slot(d, 1 - c, h), s_part.at[d, h], r_part.at[d, h], partner
        )

    greet([partner] + [dev(d) for d in near])
    take = pltpu.make_async_copy(feats, held, own_sem.at[0])
    take.start()
    for n in range(2):
        for d in near:
            own(d, (n + (d == 2)) % 2).start()
    for h in range(2):
        fwd(0, h).start()
    take.wait()
    put = pltpu.make_async_copy(held, out.at[pl.ds(r * nb, nb)], own_sem.at[1])
    put.start()
    for n in range(2):
        for d in near:
            h = (n + (d == 2)) % 2
            inc(d, h).wait_recv()
            if relay and n == 0:
                pass_on(h).start()
            fwd(d, h).start()
    if relay:
        for h in range(2):
            inc(3, h).wait_recv()
            fwd(3, h).start()
    for d in range(chips):
        for h in range(2):
            inc_part(d, h).wait_recv()
    for h in range(2):
        for d in near:
            own(d, h).wait_send()
        if relay:
            pass_on(h).wait_send()
        for d in range(chips):
            fwd(d, h).wait_send()
    put.wait()


def tile_kernel(
    back, group, blk, ncol, counts, rows, cols, tiles, src, out, lists, lens, acc
):
    slots, size = tiles.shape[0], tiles.shape[1]
    dests = out.shape[0]
    span = blk * ncol

    def row_id(k):
        return rows[k] % span

    def col_id(k):
        g = cols[k]
        return g // span * blk + g % blk

    dst_of, src_of = (col_id, row_id) if back else (row_id, col_id)

    @pl.loop(0, dests)
    def _(d):
        lens[d] = 0

    @pl.loop(0, counts[0])
    def _(k):
        d = dst_of(k)
        n = lens[d]
        lists[d * slots + n] = k
        lens[d] = n + 1

    def product(d, m, t):
        left, right = [], []
        for i in range(group):
            at = t * group + i
            k = jnp.where(at < m, lists[d * slots + jnp.minimum(at, slots - 1)], 0)
            mat = tiles[k]
            left.append(jnp.where(at < m, mat, jnp.zeros_like(mat)))
            right.append(src[src_of(k)])
        lhs = jnp.concatenate(left, axis=0 if back else 1)
        rhs = jnp.concatenate(right, axis=0)
        dims = (((0,), (0,)), ((), ())) if back else (((1,), (0,)), ((), ()))
        return lax.dot_general(lhs, rhs, dims, preferred_element_type=F32)

    @pl.loop(0, dests // WAYS)
    def _(e):
        ids = [e * WAYS + i for i in range(WAYS)]
        sizes = [lens[d] for d in ids]
        most = functools.reduce(jnp.maximum, sizes)
        for i in range(WAYS):
            acc[i] = product(ids[i], sizes[i], 0)

        @pl.loop(1, (most + group - 1) // group)
        def _(t):
            for i in range(WAYS):
                acc[i] = acc[i] + product(ids[i], sizes[i], t)

        for i in range(WAYS):
            out[ids[i]] = acc[i].astype(BF)


def middle_kernel(
    n, chips, np_, scale, part, w, bias, cot, out, spread, ws,
    acc_r, acc_l, agg, gp, accf, wp, w1, w2,
    s_r, r_r, s_l, r_l, s_gr, r_gr, s_gl, r_gl, s_w1, r_w1, s_w2, r_w2,
):
    r, q = lax.axis_index("row"), lax.axis_index("col")
    k, c = r // 2, r % 2
    last = n - 1
    right, left = (r, jnp.minimum(q + 1, last)), (r, jnp.maximum(q - 1, 0))
    partner = (k * 2 + 1 - c, q)
    size = part.shape[1]

    def dev(d):
        return (flip(k, d) * 2 + c, q)

    def chain(buf, s, v, to, d, j, first=False):
        at = d * np_ + j
        return remote(
            (part if first else buf).at[at], buf.at[at], s.at[d, j], v.at[d, j], to
        )

    cp_r = functools.partial(chain, acc_r, s_r, r_r, right)
    cp_l = functools.partial(chain, acc_l, s_l, r_l, left)

    def cp_g(s, v, to, d, j):
        at = d * np_ + j
        return remote(spread.at[at], spread.at[at], s.at[d, j], v.at[d, j], to)

    cp_gr = functools.partial(cp_g, s_gr, r_gr, right)
    cp_gl = functools.partial(cp_g, s_gl, r_gl, left)
    cp_w1 = remote(wp.at[1 - c], w1, s_w1.at[0], r_w1.at[0], partner)

    def cp_w2(d):
        return remote(w1.at[flip(k, d)], w2.at[d], s_w2.at[d], r_w2.at[d], dev(d))

    def hop(cp, buf, start, d, j):
        @pl.when(start)
        def _():
            cp(d, j, True).start()

        @pl.when(jnp.logical_not(start))
        def _():
            cp(d, j).wait_recv()
            at = d * np_ + j
            buf[at] = (buf[at].astype(F32) + part[at].astype(F32)).astype(BF)
            cp(d, j).start()

    def live(j):
        return jnp.logical_and(j >= 0, j < np_)

    def reduce_step(t):
        jr, jl = t - q, t - (last - q)

        @pl.when(live(jr))
        def _():
            @pl.loop(0, last - q)
            def _(i):
                hop(cp_r, acc_r, q == 0, last - i, jr)

        @pl.when(live(jl))
        def _():
            @pl.loop(0, q)
            def _(i):
                hop(cp_l, acc_l, q == last, i, jl)

    def finish(j):
        at = q * np_ + j
        accf[...] = part[at].astype(F32)

        @pl.when(q > 0)
        def _():
            cp_r(q, j).wait_recv()
            accf[...] += acc_r[at].astype(F32)

        @pl.when(q < last)
        def _():
            cp_l(q, j).wait_recv()
            accf[...] += acc_l[at].astype(F32)

        rows = pl.ds(pl.multiple_of(j * size, size), size)
        a = accf[...].astype(BF)
        agg[rows, :] = a
        pre = jnp.dot(a, w[...], preferred_element_type=F32) + bias[...]
        sig = jax.nn.sigmoid(pre)
        out[rows, :] = (pre * sig).astype(BF)
        g = (cot[rows, :].astype(F32) * sig * (1.0 + pre * (1.0 - sig))).astype(BF)
        gp[rows, :] = g
        spread[at] = lax.dot_general(
            g, w[...], (((1,), (1,)), ((), ())), preferred_element_type=F32
        ).astype(BF)

        @pl.when(q < last)
        def _():
            cp_gr(q, j).start()

        @pl.when(q > 0)
        def _():
            cp_gl(q, j).start()

    def relay(j, o):
        @pl.when(jnp.logical_and(live(j), q >= o))
        def _():
            cp_gr(q - o, j).wait_recv()

            @pl.when(q < last)
            def _():
                cp_gr(q - o, j).start()

        @pl.when(jnp.logical_and(live(j), q + o <= last))
        def _():
            cp_gl(q + o, j).wait_recv()

            @pl.when(q > 0)
            def _():
                cp_gl(q + o, j).start()

    barrier = pltpu.get_barrier_semaphore()
    peers = [partner] + [dev(d) for d in range(1, chips)]
    for peer in peers:
        pl.semaphore_signal(barrier, inc=1, device_id=peer, device_id_type=MESH)

    @pl.when(q > 0)
    def _():
        pl.semaphore_signal(barrier, inc=1, device_id=left, device_id_type=MESH)

    @pl.when(q < last)
    def _():
        pl.semaphore_signal(barrier, inc=1, device_id=right, device_id_type=MESH)

    pl.semaphore_wait(barrier, jnp.minimum(q, 1) + jnp.minimum(last - q, 1) + len(peers))

    @pl.loop(0, np_ + 2 * last)
    def _(t):
        reduce_step(t)
        for o in range(1, n):
            relay(t - last - o, o)

        @pl.when(live(t - last))
        def _():
            finish(t - last)

        @pl.when(t == np_ - 1 + last)
        def _():
            weight_block(chips, scale, agg, gp, wp)
            cp_w1.start()

        @pl.when(t == np_ - 1 + last + 1)
        def _():
            cp_w1.wait_recv()
            for z in range(chips):
                w1[z] = (w1[z].astype(F32) + wp[c, z].astype(F32)).astype(BF)
            for d in range(1, chips):
                cp_w2(d).start()

    total = w1[k].astype(F32)
    for d in range(1, chips):
        cp_w2(d).wait_recv()
        total = total + w2[d].astype(F32)
    ws[...] = total.astype(BF)

    @pl.loop(0, np_)
    def _(j):
        for d in range(n):
            @pl.when(q < d)
            def _():
                cp_r(d, j).wait_send()

            @pl.when(q > d)
            def _():
                cp_l(d, j).wait_send()

            @pl.when(jnp.logical_and(q >= d, q < last))
            def _():
                cp_gr(d, j).wait_send()

            @pl.when(jnp.logical_and(q <= d, q > 0))
            def _():
                cp_gl(d, j).wait_send()

    cp_w1.wait_send()
    for d in range(1, chips):
        cp_w2(d).wait_send()


def weight_block(parts, scale, agg, gp, wp):
    width = agg.shape[1]
    rows = width // (2 * parts)
    total = jnp.sum(gp[...].astype(F32), axis=0, keepdims=True) * scale
    pad = jnp.broadcast_to(total, (PAD, width)).astype(BF)
    step = 128
    for t in range(width // step):
        res = lax.dot_general(
            agg[:, t * step : (t + 1) * step],
            gp[...],
            (((0,), (0,)), ((), ())),
            preferred_element_type=F32,
        )
        res = (res * scale).astype(BF)
        for u in range(step // rows):
            p = (t * step) // rows + u
            wp[p // parts, p % parts, :rows, :] = res[u * rows : (u + 1) * rows]
            wp[p // parts, p % parts, rows:, :] = pad


def add_rows(dst, srcs, begin, count):
    step = 64

    @pl.loop(0, count // step)
    def _(i):
        at = pl.ds(pl.multiple_of(begin + i * step, step), step)
        total = srcs[0][at, :].astype(F32)
        for s in srcs[1:]:
            total = total + s[at, :].astype(F32)
        dst[at, :] = total.astype(dst.dtype)


def final_kernel(
    chips, n, part, ws, fg, w4, bg, a_buf, b_buf, c_buf, w3,
    s_a, r_a, s_b, r_b, s_c, r_c, s_w3, r_w3, s_w4, r_w4, s_w5, r_w5,
):
    r, q = lax.axis_index("row"), lax.axis_index("col")
    k, c = r // 2, r % 2
    relay = chips == 4
    near = [d for d in range(1, chips) if not (relay and d == 3)]
    partner = (k * 2 + 1 - c, q)
    rows = part.shape[1]
    half = rows // 2

    def dev(d):
        return (flip(k, d) * 2 + c, q)

    def deep(dz):
        return (r, (q + dz) % n)

    def mine(d):
        return part.at[flip(k, d) * 2 + c]

    def cp_a(d):
        return remote(
            part.at[flip(k, d) * 2 + 1 - c], a_buf.at[d], s_a.at[d], r_a.at[d], partner
        )

    def cp_b(d, h):
        at = pl.ds(h * half, half)
        return remote(a_buf.at[d, at], b_buf.at[d, at], s_b.at[d, h], r_b.at[d, h], dev(d))

    def cp_c(h):
        return remote(
            a_buf.at[3, pl.ds(h * half, half)], c_buf.at[h], s_c.at[h], r_c.at[h], dev(h + 1)
        )

    def cp_w3(dz):
        return remote(ws, w3.at[q], s_w3.at[dz], r_w3.at[dz], deep(dz))

    def cp_w4(d):
        return remote(w4.at[c, k], w4.at[c, k], s_w4.at[d], r_w4.at[d], dev(d))

    def cp_w5(d):
        at = flip(k, d)
        return remote(w4.at[c, at], w4.at[c, at], s_w5.at[d], r_w5.at[d], partner)

    greet([partner] + [dev(d) for d in range(1, chips)] + [deep(dz) for dz in range(1, n)])
    order = list(range(chips - 1, 0, -1)) + [0]
    if relay:
        order = [3, 1, 2, 0]
    for d in order:
        cp_a(d).start()
    for dz in range(1, n):
        cp_w3(dz).start()

    def join(d):
        cp_a(d).wait_recv()
        add_rows(a_buf.at[d], [a_buf.at[d], mine(d)], 0, rows)

    if relay:
        join(3)
        cp_c(0).start()
        cp_c(1).start()
        join(1)
        cp_b(1, 0).start()
        join(2)
        cp_b(2, 1).start()
    else:
        for d in order[:-1]:
            join(d)
            for h in range(2):
                cp_b(d, h).start()

    w3[q] = ws[...]
    for dz in range(1, n):
        at = (q + n - dz) % n
        remote(w3.at[at], w3.at[at], s_w3.at[dz], r_w3.at[dz], deep(dz)).wait_recv()
    total = w3[0].astype(F32)
    for i in range(1, n):
        total = total + w3[i].astype(F32)
    w4[c, k] = total.astype(BF)
    for d in range(1, chips):
        cp_w4(d).start()
    cp_w5(0).start()

    if relay:
        cp_c(0).wait_recv()
        add_rows(a_buf.at[2], [a_buf.at[2], c_buf.at[0]], 0, half)
        cp_b(2, 0).start()
        cp_c(1).wait_recv()
        at = pl.ds(half, half)
        add_rows(a_buf.at[1, at], [a_buf.at[1, at], c_buf.at[1]], 0, half)
        cp_b(1, 1).start()

    join(0)
    for d in range(1, chips):
        at = flip(k, d)
        remote(w4.at[c, at], w4.at[c, at], s_w4.at[d], r_w4.at[d], dev(d)).wait_recv()
        cp_w5(d).start()
    for h in range(2):
        for d in near:
            cp_b(d, (h + (d == 2)) % 2).wait_recv()
    add_rows(fg, [a_buf.at[0]] + [b_buf.at[d] for d in near], 0, rows)

    for d in range(chips):
        at = flip(k, d)
        remote(
            w4.at[1 - c, at], w4.at[1 - c, at], s_w5.at[d], r_w5.at[d], partner
        ).wait_recv()

    bg[...] = w4[0, 0, w4.shape[2] - PAD :, :].astype(F32)[:1]
    for d in range(chips):
        cp_a(d).wait_send()
        cp_w5(d).wait_send()
    for d in near:
        for h in range(2):
            cp_b(d, h).wait_send()
    if relay:
        for h in range(2):
            cp_c(h).wait_send()
    for d in range(1, chips):
        cp_w4(d).wait_send()
    for dz in range(1, n):
        cp_w3(dz).wait_send()


VM = pl.BlockSpec(memory_space=pltpu.VMEM)
SM = pl.BlockSpec(memory_space=pltpu.SMEM)
ANY = pl.BlockSpec(memory_space=pl.ANY)


def params(cid):
    return pltpu.CompilerParams(collective_id=cid, has_side_effects=True)


def dma(*shape):
    return pltpu.SemaphoreType.DMA(shape)


def run_tiles(back, group, blk, ncol, dests, counts, rows, cols, values, src):
    slots, size = values.shape[0], values.shape[1]
    width = src.shape[2]
    return pl.pallas_call(
        functools.partial(tile_kernel, back, group, blk, ncol),
        out_shape=jax.ShapeDtypeStruct((dests, size, width), BF),
        in_specs=[SM, SM, SM, VM, VM],
        out_specs=VM,
        scratch_shapes=[
            pltpu.SMEM((dests * slots,), jnp.int32),
            pltpu.SMEM((dests,), jnp.int32),
            pltpu.VMEM((WAYS, size, width), F32),
        ],
        name="tiles_back" if back else "tiles_fwd",
    )(counts, rows, cols, values, src)


def on_device(features, weight, bias, cotangent, tile_values, tile_rows, tile_cols, tile_counts):
    nrow = lax.axis_size("row")
    ncol = lax.axis_size("col")
    node_dev, width = features.shape
    slots, size = tile_values.shape[2], tile_values.shape[3]
    nb = node_dev // size
    chips = nrow // 2
    scale = 1.0 / math.sqrt(node_dev * nrow * ncol)
    values = tile_values.reshape(slots, size, size)
    rows, cols = tile_rows.reshape(slots), tile_cols.reshape(slots)
    counts = tile_counts.reshape(1)

    gathered = pl.pallas_call(
        functools.partial(gather_kernel, chips, nb),
        out_shape=jax.ShapeDtypeStruct((nrow * nb, size, width), BF),
        in_specs=[ANY],
        out_specs=ANY,
        scratch_shapes=[pltpu.VMEM((nb, size, width), BF), dma(2)] + [dma(chips, 2)] * 4,
        compiler_params=params(0),
        name="gather",
    )(features.reshape(nb, size, width))

    partial = run_tiles(False, 4, nb, ncol, ncol * nb, counts, rows, cols, values, gathered)

    part_rows = width // (2 * chips)
    pr = part_rows + PAD
    piece = size // 2
    pieces = node_dev // piece
    wide = (ncol * pieces, piece, width)
    out, spread, ws = pl.pallas_call(
        functools.partial(middle_kernel, ncol, chips, pieces, scale),
        out_shape=[
            jax.ShapeDtypeStruct((node_dev, width), BF),
            jax.ShapeDtypeStruct(wide, BF),
            jax.ShapeDtypeStruct((pr, width), BF),
        ],
        in_specs=[VM] * 4,
        out_specs=[VM] * 3,
        scratch_shapes=[
            pltpu.VMEM(wide, BF),
            pltpu.VMEM(wide, BF),
            pltpu.VMEM((node_dev, width), BF),
            pltpu.VMEM((node_dev, width), BF),
            pltpu.VMEM((piece, width), F32),
            pltpu.VMEM((2, chips, pr, width), BF),
            pltpu.VMEM((chips, pr, width), BF),
            pltpu.VMEM((chips, pr, width), BF),
        ]
        + [dma(ncol, pieces)] * 8
        + [dma(1), dma(1), dma(chips), dma(chips)],
        compiler_params=params(1),
        name="middle",
    )(partial.reshape(wide), weight, bias.reshape(1, width), cotangent)
    spread = spread.reshape(ncol * nb, size, width)

    grads = run_tiles(True, 2, nb, ncol, nrow * nb, counts, rows, cols, values, spread)

    fg, parts, bg = pl.pallas_call(
        functools.partial(final_kernel, chips, ncol),
        out_shape=[
            jax.ShapeDtypeStruct((node_dev, width), BF),
            jax.ShapeDtypeStruct((2, chips, pr, width), BF),
            jax.ShapeDtypeStruct((1, width), F32),
        ],
        in_specs=[VM] * 2,
        out_specs=[VM] * 3,
        scratch_shapes=[
            pltpu.VMEM((chips, node_dev, width), BF),
            pltpu.VMEM((chips, node_dev, width), BF),
            pltpu.VMEM((2, node_dev // 2, width), BF),
            pltpu.VMEM((ncol, pr, width), BF),
            dma(chips), dma(chips), dma(chips, 2), dma(chips, 2), dma(2), dma(2),
            dma(ncol), dma(ncol), dma(chips), dma(chips), dma(chips), dma(chips),
        ],
        compiler_params=params(2),
        name="final",
    )(grads.reshape(nrow, node_dev, width), ws)
    wg = parts[:, :, :part_rows].astype(F32).reshape(width, width)
    return (out, fg, wg, bg.reshape(width))


def solution(mesh):
    return jax.shard_map(
        on_device,
        mesh=mesh,
        in_specs=(
            P(("row", "col"), None),
            P(),
            P(),
            P(("row", "col"), None),
            P("row", "col", None, None, None),
            P("row", "col", None),
            P("row", "col", None),
            P("row", "col"),
        ),
        out_specs=(P(("row", "col"), None), P(("row", "col"), None), P(), P()),
        check_vma=False,
    )
```
